32 devices in a mesh: space: 8 (over z, x), snap: 4 (over y, core).
Axes of the slice: x: 2, y: 2, z: 4, core: 2. Of those that a mesh axis runs over, the one named last changes fastest.
Arguments:
- snapshots: bfloat16 [131072, 512], P('space', 'snap'), may hold values from -6 to 6
- mass_blocks: bfloat16 [1024, 3, 128, 128], P(('space', 'snap')), may hold values from -0.3125 to 0.3125
- neighbours: int32 [1024, 3], P(('space', 'snap')), may hold values from 0 to 1023, as said below
- eigvecs: bfloat16 [512, 128], replicated, may hold values from -0.25 to 0.25
Outputs:
- weighted: bfloat16 [131072, 512], P(('space', 'snap'))
- correlation: float32 [512, 512], P('snap', 'space')
- modes: bfloat16 [131072, 128], P(('space', 'snap'))
The draws below stay inside these ranges and needn't reach their ends.
Inputs may be any that keep to these rules, and one draw needn't show every extreme that they name: neighbours[b, 0] is b; every entry lies within 4 of b; neighbours[b, 2] lies exactly 4 away from b.
All inputs are finite; a program needn't handle non-finite values.
Results may differ from the reference program's by a relative error of at most 0.0029.
Values may be sent and summed in bfloat16 or wider, within the bound.
A program may use at most 128 MiB of HBM per device.

```python
import jax
import jax.numpy as jnp
from jax import lax

SNAPS = 512
MODES = 128
BLOCK = 128
NB = 3
HB = 4
NCELLS = 131072
NBLK = 1024


def draw_neighbours(key, part):
    block_ids = jnp.arange(NBLK, dtype=jnp.int32)
    key_one, key_two, key_three = jax.random.split(key, 3)
    reach_one = jax.random.randint(key_one, (NBLK,), 1, HB + 1, dtype=jnp.int32)
    sign_one = jax.random.randint(key_two, (NBLK,), 0, 2, dtype=jnp.int32) * 2 - 1
    sign_two = jax.random.randint(key_three, (NBLK,), 0, 2, dtype=jnp.int32) * 2 - 1

    def mirror(reach, sign):
        target = block_ids + sign * reach
        outside = (target < 0) | (target >= NBLK)
        return jnp.where(outside, block_ids - sign * reach, target)
    far_reach = jnp.full((NBLK,), HB, dtype=jnp.int32)
    return jnp.stack([block_ids, mirror(reach_one, sign_one), mirror(far_reach, sign_two)], axis=1).astype(jnp.int32)


def block_levels(stream_key, extent, cuts, smallest, largest):
    level, own = 1.0, jax.random.fold_in(stream_key, 6)
    for position, blocks in cuts:
        draws = jnp.exp(jax.random.uniform(jax.random.fold_in(own, position), (blocks,), jnp.float32, smallest / len(cuts), largest / len(cuts)))
        level = level * jnp.repeat(draws, extent[position] // blocks).reshape([-1 if axis == position else 1 for axis in range(len(extent))])
    return level


def bell_draw(rng, dims, spread, bound, cuts=(), kind=jnp.bfloat16):
    result = spread * jax.random.normal(rng, dims, jnp.float32)
    if cuts:
        result = result * block_levels(rng, dims, cuts, -0.22, 0.18)
    return jnp.clip(result, -bound, bound).astype(kind)


def setup_inputs(seed: int = 0) -> dict:
    seeds = jax.random.split(jax.random.key(seed), 5)
    snapshots = bell_draw(seeds[0], (NCELLS, SNAPS), 1.0, 6.0, ((0, 8), (1, 4)))
    mass_blocks = bell_draw(seeds[1], (NBLK, NB, BLOCK, BLOCK), (NB * BLOCK) ** -0.5, 0.3125, ((0, 32),))
    neighbours = draw_neighbours(jax.random.fold_in(seeds[4], 71), 0)
    eigvecs = bell_draw(seeds[3], (SNAPS, MODES), SNAPS ** -0.5, 0.25)
    return dict(snapshots=snapshots, mass_blocks=mass_blocks, neighbours=neighbours, eigvecs=eigvecs)


group_size = 32


def reference(snapshots, mass_blocks, neighbours, eigvecs):
    blocks = snapshots.reshape(NBLK, BLOCK, SNAPS)

    def weigh(packed):
        mass_part, block_ids = packed
        nearby = blocks[block_ids].astype(jnp.float32)
        return jnp.einsum("bjrc,bjcs->brs", mass_part.astype(jnp.float32), nearby)

    stacked = lax.map(weigh, (mass_blocks.reshape(-1, group_size, NB, BLOCK, BLOCK), neighbours.reshape(-1, group_size, NB)))
    weighted = stacked.reshape(NCELLS, SNAPS).astype(jnp.bfloat16)
    correlation = jnp.dot(weighted.T, snapshots, preferred_element_type=jnp.float32) * (1.0 / NCELLS)
    modes = jnp.dot(snapshots, eigvecs, preferred_element_type=jnp.float32).astype(jnp.bfloat16)
    return weighted, correlation, modes
```

```python
import functools

import jax
import jax.numpy as jnp
from jax import lax
from jax.experimental import pallas as pl
from jax.experimental.pallas import tpu as pltpu
from jax.sharding import PartitionSpec as P

HB = 4
MESH = pl.DeviceIdType.MESH
BF16 = jnp.bfloat16
F32 = jnp.float32


def transposed_dot(left, right):
    return lax.dot_general(left, right, (((0,), (0,)), ((), ())), preferred_element_type=F32)


def fused(n, ns, scale, near_hbm, src, mass_hbm, eig_hbm, weighted, modes, corr_out,
          base, far, win, mass, eig, near, acc, tiles, recv,
          loc, send_own, recv_own, recv_rim, send_far, recv_far, send_out, fwd_sems, tile_sems,
          gate, sync):
    nz = ns // 2
    s, k = lax.axis_index("space"), lax.axis_index("snap")
    y, c, z, x = k // 2, k % 2, s // 2, s % 2
    yo = 1 - y
    partner = 2 * y + 1 - c
    blocks, size, width = src.shape
    own_blocks = blocks // n
    chip_blocks = 2 * own_blocks
    pieces = own_blocks // HB
    rim = HB * size
    picks = mass.shape[1]
    top = HB + own_blocks
    first_block = (s * n + k) * own_blocks - HB
    lanes_own = pl.multiple_of(2 * y * width, 2 * width)
    lanes_far = [pl.multiple_of((2 * yo + i) * width, width) for i in range(2)]

    def local(i, origin, target):
        return pltpu.make_async_copy(origin, target, loc.at[i])

    def remote(origin, target, sends, recvs, device):
        return pltpu.make_async_remote_copy(src_ref=origin, dst_ref=target, send_sem=sends,
                                            recv_sem=recvs, device_id=device, device_id_type=MESH)

    def rows_of(first, count):
        return src.at[pl.ds(first, count)]

    def greet(sem):
        for t in range(1, n):
            pl.semaphore_signal(sem, inc=1, device_id=(s, lax.rem(k + t, n)), device_id_type=MESH)
        pl.semaphore_signal(sem, inc=1, device_id=(2 * z + 1 - x, k), device_id_type=MESH)

        @pl.when(z > 0)
        def _():
            pl.semaphore_signal(sem, inc=1, device_id=(s - 2, k), device_id_type=MESH)

        @pl.when(z < nz - 1)
        def _():
            pl.semaphore_signal(sem, inc=1, device_id=(s + 2, k), device_id_type=MESH)

        pl.semaphore_wait(sem, n + jnp.where(z > 0, 1, 0) + jnp.where(z < nz - 1, 1, 0))

    edge = c != y
    outer = edge | ((y == 0) & (s > 0)) | ((y == 1) & (s < ns - 1))
    cross_rim = ((y == 0) & (s > 0)) | ((y == 1) & (s < ns - 1))
    plane_rim = ((y == 0) & (s < ns - 1)) | ((y == 1) & (s > 0))

    keep = local(0, rows_of(y * chip_blocks + c * (own_blocks - HB), own_blocks + HB),
                 base.at[c, pl.ds((1 - c) * HB, own_blocks + HB)])
    edge_rows = rows_of(chip_blocks - y * HB, HB)
    edge_keep = local(1, edge_rows, base.at[c, pl.ds(yo * top, HB)])
    fetch = local(2, mass_hbm, mass)
    fetch_eig = local(3, eig_hbm, eig)
    fetch_near = local(4, near_hbm, near)

    mains = []
    for o in range(pieces):
        for co in range(2):
            at = yo * chip_blocks + ((pieces - 1 - o) * HB if co == 0 else own_blocks + o * HB)
            to = (pieces - o) * HB if co == 0 else (1 + o) * HB
            mains.append(remote(rows_of(at, HB), far.at[c, pl.ds(to, HB)], send_far.at[co, o],
                                recv_far.at[c, o + 1], (s, 2 * yo + co)))
    cross_edge = remote(rows_of(chip_blocks - yo * HB, HB), far.at[c, pl.ds(y * top, HB)],
                        send_out.at[0], recv_far.at[c, pieces + 1], (s, 2 * yo + y))
    cross = remote(rows_of(y * (blocks - HB), HB), far.at[c, pl.ds(yo * top, HB)],
                   send_out.at[1], recv_far.at[c, pieces + 1], (s + 2 * y - 1, yo * (n - 1)))
    plane = remote(rows_of(yo * (blocks - HB), HB), base.at[c, pl.ds(y * top, HB)],
                   send_out.at[2], recv_rim.at[c], (s + 1 - 2 * y, y * (n - 1)))
    plane_edge = remote(edge_rows, base.at[c, pl.ds(yo * top, HB)], send_out.at[3], recv_rim.at[c],
                        (s, partner))
    own = remote(rows_of(y * chip_blocks + (1 - c) * (own_blocks - HB), own_blocks + HB),
                 base.at[c, pl.ds(c * HB, own_blocks + HB)], send_own, recv_own, (s, partner))

    keep.start()
    pl.when(edge)(edge_keep.start)
    fetch_near.start()
    fetch.start()
    fetch_eig.start()

    greet(pltpu.get_barrier_semaphore())

    @pl.when(c == 0)
    def _():
        for copy in mains:
            copy.start()
        cross_edge.start()

    own.start()
    pl.when(jnp.logical_not(edge))(plane_edge.start)
    acc[...] = jnp.zeros_like(acc)
    for i in range(nz + 1):
        greet(sync.at[i])
    pl.when(plane_rim)(plane.start)
    pl.when(cross_rim & (c == 0))(cross.start)

    def wait_rim(buffer, index, recvs):
        remote(buffer.at[index, pl.ds(0, HB)], buffer.at[index, pl.ds(0, HB)], send_own, recvs,
               (s, partner)).wait_recv()

    def masses_of(row):
        return jnp.concatenate([mass[row, j] for j in range(picks)], axis=1)

    def place_of(row, j):
        return jnp.clip(near[j, row] - first_block, 0, base.shape[1] - 1)

    me = s * n + k

    def send_block(j, i):
        column = 2 * y + j if j < 2 else 2 * yo + j - 2
        band = 2 * y + i if i < 2 else 2 * yo + i - 2
        value = acc[j * width:(j + 1) * width, i * width:(i + 1) * width].astype(BF16)
        tiles[i, j] = value.reshape(tiles.shape[2:])
        for half in range(2):
            target = 2 * column + half
            mine = (target == s) & (band == k)
            copy = remote(tiles.at[i, j, half], recv.at[me], tile_sems.at[0], tile_sems.at[1],
                          (target, band))
            pl.when(jnp.logical_not(mine))(copy.start)

            @pl.when(mine)
            def _():
                recv[me] = tiles[i, j, half]

    keep.wait()
    own.wait_recv()
    pl.when(edge)(edge_keep.wait)
    for i in range(2):
        @pl.when(outer & (jnp.logical_not(edge) | (c != i)))
        def _():
            wait_rim(base, i, recv_rim.at[i])
    fetch.wait()
    fetch_near.wait()

    def held(buffer, index, slot):
        return buffer[index, pl.ds(pl.multiple_of(slot * HB, HB), HB)].reshape(rim, width)

    def near_fields(slot):
        return jnp.concatenate([held(base, 0, slot), held(base, 1, slot)], axis=1)

    @pl.loop(0, pieces)
    def _(group):
        for i in range(HB):
            row = group * HB + i
            places = [place_of(row, j) for j in range(picks)]
            fields = jnp.concatenate(
                [jnp.concatenate([base[half, place] for place in places], axis=0) for half in range(2)],
                axis=1)
            product = jnp.dot(masses_of(row), fields, preferred_element_type=F32)
            weighted[pl.ds(pl.multiple_of(row * size, size), size), pl.ds(lanes_own, 2 * width)] = (
                product.astype(BF16))
        rows = pl.ds(pl.multiple_of(group * rim, rim), rim)
        acc[0:2 * width, 0:2 * width] += transposed_dot(
            near_fields(group + 1), weighted[rows, pl.ds(lanes_own, 2 * width)])

    for j in range(2):
        for i in range(2):
            send_block(j, i)
    fetch_eig.wait()

    def slot_of(order):
        return jnp.where(c == 1, order, pieces + 1 - order)

    def phase(index):
        lanes = lanes_far[index]
        known = (2 + index) * width

        def rows_at(order):
            return pl.ds(pl.multiple_of((slot_of(order) - 1) * rim, rim), rim)

        def admit(order):
            first = pl.multiple_of(slot_of(order) * HB, HB)
            win[pl.ds(first, HB)] = far[index, pl.ds(first, HB)]

        def gathered(order, count):
            slot = slot_of(order)
            parts = [held(base, 0, slot), held(base, 1, slot)]
            return jnp.concatenate(parts + [held(far, i, slot) for i in range(count)], axis=1)

        def meet(order):
            rows = rows_at(order)
            parts = [weighted[rows, pl.ds(lanes_own, 2 * width)]]
            parts += [weighted[rows, pl.ds(lanes_far[i], width)] for i in range(index)]
            earlier = jnp.concatenate(parts, axis=1) if index else parts[0]
            acc[known:known + width, 0:known] += transposed_dot(
                held(far, index, slot_of(order)), earlier)
            if index == 1:
                vectors = jnp.concatenate(
                    [eig[pl.ds(lanes_own, 2 * width)]] + [eig[pl.ds(lanes_far[i], width)] for i in range(2)],
                    axis=0)
                modes[rows, :] = jnp.dot(gathered(order, 2), vectors,
                                         preferred_element_type=F32).astype(BF16)

        def work(order):
            slot = slot_of(order)
            for i in range(HB):
                row = (slot - 1) * HB + i
                fields = jnp.concatenate([win[place_of(row, j)] for j in range(picks)], axis=0)
                product = jnp.dot(masses_of(row), fields, preferred_element_type=F32)
                weighted[pl.ds(pl.multiple_of(row * size, size), size), pl.ds(lanes, width)] = (
                    product.astype(BF16))
            acc[0:known + width, known:known + width] += transposed_dot(
                gathered(order, index + 1), weighted[rows_at(order), pl.ds(lanes, width)])

        wait_rim(far, index, recv_far.at[index, 1])
        mid = far.at[index, pl.ds(slot_of(1) * HB, HB)]
        forward = remote(mid, far.at[index, pl.ds(c * top, HB)], fwd_sems.at[index],
                         recv_far.at[index, 0], (s, partner))
        forward.start()
        admit(1)
        meet(1)
        wait_rim(far, index, recv_far.at[index, 0])
        admit(0)

        @pl.loop(0, pieces - 1)
        def _(p):
            wait_rim(far, index, recv_far.at[index, p + 2])
            admit(p + 2)
            meet(p + 2)
            if index == 0:
                ready = p == pieces - 3

                @pl.when(ready & (c == 0))
                def _():
                    for co in range(2):
                        mains[2 * (pieces - 4) + co].wait_send()
                    pl.semaphore_signal(gate, inc=1, device_id=(s, partner), device_id_type=MESH)

                @pl.when(ready & (c == 1))
                def _():
                    pl.semaphore_wait(gate, 1)
                    for copy in mains:
                        copy.start()
                    cross_edge.start()
                    pl.when(cross_rim)(cross.start)
            work(p + 1)

        for i in range(2 + index):
            send_block(2 + index, i)

        @pl.when(outer)
        def _():
            wait_rim(far, index, recv_far.at[index, pieces + 1])
        admit(pieces + 1)
        work(pieces)
        for j in range(3 + index):
            send_block(j, 2 + index)
        forward.wait_send()

    phase(0)
    phase(1)

    for i, copy in enumerate(mains):
        if i // 2 == pieces - 4:
            pl.when(c == 1)(copy.wait_send)
        else:
            copy.wait_send()
    cross_edge.wait_send()
    own.wait_send()
    pl.when(jnp.logical_not(edge))(plane_edge.wait_send)
    pl.when(plane_rim)(plane.wait_send)
    pl.when(cross_rim)(cross.wait_send)
    others = recv.at[pl.ds(0, n * ns - 1)]
    remote(others, others, tile_sems.at[0], tile_sems.at[1], (s, partner)).wait()
    total = recv[0].astype(F32)
    for i in range(1, n * ns):
        total = total + recv[i].astype(F32)
    corr_out[...] = total * scale


def deliver(weighted, modes, corr, weighted_out, modes_out, corr_out, sems):
    parts = sems.shape[0] // 2 - 1
    pairs = [(corr, corr_out)]
    for held, target in ((weighted, weighted_out), (modes, modes_out)):
        rows = held.shape[0] // parts
        pairs += [(held.at[pl.ds(i * rows, rows)], target.at[pl.ds(i * rows, rows)]) for i in range(parts)]
    copies = [pltpu.make_async_copy(held, target, sems.at[i]) for i, (held, target) in enumerate(pairs)]
    for copy in copies:
        copy.start()
    for copy in copies:
        copy.wait()


def fast_shards(n, ns, snapshots, mass_blocks, neighbours, eigvecs):
    own_blocks, picks, size, _ = mass_blocks.shape
    total, width = snapshots.shape
    rows = total // n
    snaps = n * width
    pieces = own_blocks // HB
    sem = pltpu.SemaphoreType.DMA
    regular = pltpu.SemaphoreType.REGULAR
    vmem = pltpu.VMEM
    nz = ns // 2
    tile = snaps // ns
    held = own_blocks + 2 * HB
    modes_count = eigvecs.shape[1]
    hbm = pl.BlockSpec(memory_space=pltpu.HBM)
    inside = pl.BlockSpec(memory_space=pltpu.VMEM)
    block = (size, width)
    weighted, modes, corr = pl.pallas_call(
        functools.partial(fused, n, ns, 1.0 / (total * ns)),
        out_shape=(jax.ShapeDtypeStruct((rows, snaps), BF16),
                   jax.ShapeDtypeStruct((rows, modes_count), BF16),
                   jax.ShapeDtypeStruct((tile, width), F32)),
        in_specs=[hbm] * 4,
        out_specs=(inside, inside, inside),
        scratch_shapes=[
            vmem((2, held) + block, BF16), vmem((2, held) + block, BF16), vmem((held,) + block, BF16),
            vmem(mass_blocks.shape, BF16), vmem(eigvecs.shape, BF16),
            pltpu.SMEM((picks, own_blocks), jnp.int32), vmem((snaps, snaps), F32),
            vmem((n, n, 2, tile, width), BF16), vmem((n * ns, tile, width), BF16),
            sem((5,)), sem, sem, sem((2,)), sem((2, pieces)), sem((2, pieces + 2)), sem((4,)), sem((2,)),
            sem((2,)), regular, regular((nz + 1,)),
        ],
        compiler_params=pltpu.CompilerParams(collective_id=0, has_side_effects=True,
                                             vmem_limit_bytes=40 * 2**20),
        name="fused",
    )(*(pltpu.with_memory_space_constraint(a, pltpu.HBM) for a in (
        neighbours.T, snapshots.reshape(total // size, size, width), mass_blocks, eigvecs)))
    weighted, modes, corr = pl.pallas_call(
        deliver,
        out_shape=tuple(pltpu.HBM(a.shape, a.dtype) for a in (weighted, modes, corr)),
        in_specs=[inside] * 3,
        out_specs=(hbm,) * 3,
        scratch_shapes=[sem((10,))],
        compiler_params=pltpu.CompilerParams(vmem_limit_bytes=2**20),
        name="deliver",
    )(*(pltpu.with_memory_space_constraint(a, pltpu.VMEM) for a in (weighted, modes, corr)))
    return weighted, corr.T, modes


def shifted(block, axis, distance):
    devices = range(lax.axis_size(axis))
    route = [(i - distance, i) for i in devices if i - distance in devices]
    return lax.ppermute(block, axis, route)


def plain_shards(snapshots, mass_blocks, neighbours, eigvecs):
    local_rows = lax.all_to_all(snapshots, "snap", split_axis=0, concat_axis=1, tiled=True)
    row_count, col_count = local_rows.shape
    block_size = mass_blocks.shape[2]
    rim_rows = HB * block_size
    below_rim = shifted(local_rows[row_count - rim_rows :], ("space", "snap"), 1)
    above_rim = shifted(local_rows[:rim_rows], ("space", "snap"), -1)
    extended = jnp.concatenate([below_rim, local_rows, above_rim], axis=0).reshape(
        -1, block_size, col_count
    )
    first_block = lax.axis_index(("space", "snap")) * (row_count // block_size)
    local_ids = neighbours - first_block + HB
    nearby = extended[local_ids]
    weighted = jnp.einsum("bjrc,bjcs->brs", mass_blocks, nearby, preferred_element_type=jnp.float32)
    weighted = weighted.reshape(row_count, col_count).astype(jnp.bfloat16)
    partial_corr = jnp.dot(weighted.T, local_rows, preferred_element_type=jnp.float32)
    band = lax.psum_scatter(partial_corr, "snap", scatter_dimension=0, tiled=True)
    correlation = lax.psum_scatter(band, "space", scatter_dimension=1, tiled=True)
    cell_total = row_count * lax.axis_size("space") * lax.axis_size("snap")
    correlation = correlation * (1.0 / cell_total)
    modes = jnp.dot(local_rows, eigvecs, preferred_element_type=jnp.float32).astype(jnp.bfloat16)
    return (weighted, correlation, modes)


def solution(mesh):
    n, ns = mesh.shape["snap"], mesh.shape["space"]

    def shards(snapshots, mass_blocks, neighbours, eigvecs):
        width = snapshots.shape[1]
        own_blocks, _, size, _ = mass_blocks.shape
        rows = own_blocks * size
        whole = n == 4 and ns == 2 * n and width % 128 == 0 and width == size
        if whole and snapshots.shape[0] == n * rows and own_blocks % HB == 0 and own_blocks >= 4 * HB:
            return fast_shards(n, ns, snapshots, mass_blocks, neighbours, eigvecs)
        return plain_shards(snapshots, mass_blocks, neighbours, eigvecs)

    in_specs = (
        P("space", "snap"),
        P(("space", "snap"), None, None, None),
        P(("space", "snap"), None),
        P(),
    )
    out_specs = (P(("space", "snap"), None), P("snap", "space"), P(("space", "snap"), None))
    return jax.shard_map(shards, mesh=mesh, in_specs=in_specs, out_specs=out_specs, check_vma=False)
```

```python
import functools

import jax
import jax.numpy as jnp
from jax import lax
from jax.experimental import pallas as pl
from jax.experimental.pallas import tpu as pltpu
from jax.sharding import PartitionSpec as P

HB = 4
MESH = pl.DeviceIdType.MESH
BF16 = jnp.bfloat16
F32 = jnp.float32


def transposed_dot(left, right):
    return lax.dot_general(left, right, (((0,), (0,)), ((), ())), preferred_element_type=F32)


def fused(n, ns, scale, near_hbm, src, mass_hbm, eig_hbm, weighted, modes, corr_out,
          base, far, win, mass, eig, near, acc, late, given, given_late, tiles, recv,
          loc, send_own, recv_own, recv_rim, send_far, recv_far, send_out, fwd_sems, give_sems, take_sems,
          tile_sems, gate, sync):
    nz = ns // 2
    s, k = lax.axis_index("space"), lax.axis_index("snap")
    y, c, z, x = k // 2, k % 2, s // 2, s % 2
    yo = 1 - y
    partner = 2 * y + 1 - c
    blocks, size, width = src.shape
    own_blocks = blocks // n
    chip_blocks = 2 * own_blocks
    pieces = own_blocks // HB
    rim = HB * size
    picks = mass.shape[1]
    top = HB + own_blocks
    first_block = (s * n + k) * own_blocks - HB
    lanes_own = pl.multiple_of(2 * y * width, 2 * width)
    lanes_far = [pl.multiple_of((2 * yo + i) * width, width) for i in range(2)]

    def local(i, origin, target):
        return pltpu.make_async_copy(origin, target, loc.at[i])

    def remote(origin, target, sends, recvs, device):
        return pltpu.make_async_remote_copy(src_ref=origin, dst_ref=target, send_sem=sends,
                                            recv_sem=recvs, device_id=device, device_id_type=MESH)

    def rows_of(first, count):
        return src.at[pl.ds(first, count)]

    def hail(sem):
        for t in range(1, n):
            pl.semaphore_signal(sem, inc=1, device_id=(s, lax.rem(k + t, n)), device_id_type=MESH)
        pl.semaphore_signal(sem, inc=1, device_id=(2 * z + 1 - x, k), device_id_type=MESH)

        @pl.when(z > 0)
        def _():
            pl.semaphore_signal(sem, inc=1, device_id=(s - 2, k), device_id_type=MESH)

        @pl.when(z < nz - 1)
        def _():
            pl.semaphore_signal(sem, inc=1, device_id=(s + 2, k), device_id_type=MESH)

    def heed(sem):
        pl.semaphore_wait(sem, n + jnp.where(z > 0, 1, 0) + jnp.where(z < nz - 1, 1, 0))

    barrier = pltpu.get_barrier_semaphore()
    hail(barrier)
    edge = c != y
    outer = edge | ((y == 0) & (s > 0)) | ((y == 1) & (s < ns - 1))
    cross_rim = ((y == 0) & (s > 0)) | ((y == 1) & (s < ns - 1))
    plane_rim = ((y == 0) & (s < ns - 1)) | ((y == 1) & (s > 0))

    keep = local(0, rows_of(y * chip_blocks + c * (own_blocks - HB), own_blocks + HB),
                 base.at[c, pl.ds((1 - c) * HB, own_blocks + HB)])
    edge_rows = rows_of(chip_blocks - y * HB, HB)
    edge_keep = local(1, edge_rows, base.at[c, pl.ds(yo * top, HB)])
    fetch = local(2, mass_hbm, mass)
    fetch_eig = local(3, eig_hbm, eig)
    fetch_near = local(4, near_hbm, near)

    mains = []
    for o in range(pieces):
        for co in range(2):
            at = yo * chip_blocks + ((pieces - 1 - o) * HB if co == 0 else own_blocks + o * HB)
            to = (pieces - o) * HB if co == 0 else (1 + o) * HB
            mains.append(remote(rows_of(at, HB), far.at[c, pl.ds(to, HB)], send_far.at[jnp.where((c == 0) & (o == pieces - 4), 1, 0)] if o == pieces - 4 else send_far.at[0],
                                recv_far.at[c, o + 1], (s, 2 * yo + co)))
    def sent(count, i):
        rows = rows_of(0, count * HB)
        remote(rows, rows, send_far.at[i], recv_own, (s, partner)).wait_send()

    cross_edge = remote(rows_of(chip_blocks - yo * HB, HB), far.at[c, pl.ds(y * top, HB)],
                        send_out.at[0], recv_far.at[c, pieces + 1], (s, 2 * yo + y))
    cross = remote(rows_of(y * (blocks - HB), HB), far.at[c, pl.ds(yo * top, HB)],
                   send_out.at[1], recv_far.at[c, pieces + 1], (s + 2 * y - 1, yo * (n - 1)))
    plane = remote(rows_of(yo * (blocks - HB), HB), base.at[c, pl.ds(y * top, HB)],
                   send_out.at[2], recv_rim.at[c], (s + 1 - 2 * y, y * (n - 1)))
    plane_edge = remote(edge_rows, base.at[c, pl.ds(yo * top, HB)], send_out.at[3], recv_rim.at[c],
                        (s, partner))
    own = remote(rows_of(y * chip_blocks + (1 - c) * (own_blocks - HB), own_blocks + HB),
                 base.at[c, pl.ds(c * HB, own_blocks + HB)], send_own, recv_own, (s, partner))

    keep.start()
    pl.when(edge)(edge_keep.start)
    fetch_near.start()
    fetch.start()
    fetch_eig.start()

    acc[...] = jnp.zeros_like(acc)
    late[...] = jnp.zeros_like(late)
    heed(barrier)

    @pl.when(c == 0)
    def _():
        for copy in mains:
            copy.start()
        cross_edge.start()

    own.start()
    pl.when(jnp.logical_not(edge))(plane_edge.start)
    for i in range(nz + 1):
        hail(sync.at[i])
        heed(sync.at[i])
    pl.when(plane_rim)(plane.start)
    pl.when(cross_rim & (c == 0))(cross.start)

    def wait_rim(buffer, index, recvs):
        remote(buffer.at[index, pl.ds(0, HB)], buffer.at[index, pl.ds(0, HB)], send_own, recvs,
               (s, partner)).wait_recv()

    def masses_of(row):
        return jnp.concatenate([mass[row, j] for j in range(picks)], axis=1)

    def place_of(row, j):
        return jnp.clip(near[j, row] - first_block, 0, base.shape[1] - 1)

    def span(first, last):
        return pl.ds(first * width, (last - first) * width)

    def give(kind, order, band, first, last):
        rows = span(first, last)
        return remote(acc.at[band, rows], given.at[kind, rows], give_sems.at[3 * kind + order],
                      take_sems.at[3 * kind + order], (s, partner))

    def column_of(j):
        return 2 * y + j if j < 2 else 2 * yo + j - 2

    def pack(kind, j, value):
        tiles[kind, j] = value.astype(BF16).reshape(tiles.shape[2:])

    def send_tiles(kind, j, slot, band):
        for half in range(2):
            target = 2 * column_of(j) + half
            copy = remote(tiles.at[kind, j, half], recv.at[slot], tile_sems.at[0], tile_sems.at[1],
                          (target, band))
            if kind:
                copy.start()
                continue
            mine = target == s
            pl.when(jnp.logical_not(mine))(copy.start)

            @pl.when(mine)
            def _():
                recv[slot] = tiles[kind, j, half]

    def share_own(order, first, last):
        copy = give(0, order, 1 - c, first, last)
        copy.start()

        def finish():
            copy.wait()
            for j in range(first, last):
                rows = span(j, j + 1)
                pack(0, j, acc[c, rows] + given[0, rows])
                send_tiles(0, j, s, k)

        return finish

    def give_far(order, first, last):
        @pl.when(c == 0)
        def _():
            give(1, order, 2, first, last).start()

    def pack_far_band(order, first, last):
        @pl.when(c == 1)
        def _():
            give(1, order, 2, first, last).wait_recv()
            for j in range(first, last):
                rows = span(j, j + 1)
                pack(1, j, acc[2, rows] + given[1, rows])

    def send_far_band(first, last):
        @pl.when(c == 1)
        def _():
            for j in range(first, last):
                send_tiles(1, j, ns + s, 2 * yo)

    keep.wait()
    own.wait_recv()
    pl.when(edge)(edge_keep.wait)
    for i in range(2):
        @pl.when(outer & (jnp.logical_not(edge) | (c != i)))
        def _():
            wait_rim(base, i, recv_rim.at[i])
    fetch.wait()
    fetch_near.wait()

    def held(buffer, index, slot):
        return buffer[index, pl.ds(pl.multiple_of(slot * HB, HB), HB)].reshape(rim, width)

    def add(first, last, band, count, value):
        for i in range(count):
            acc[band + i, first * width:last * width] += value[:, i * width:(i + 1) * width]

    def near_fields(slot):
        return jnp.concatenate([held(base, 0, slot), held(base, 1, slot)], axis=1)

    @pl.loop(0, pieces)
    def _(group):
        for i in range(HB):
            row = group * HB + i
            places = [place_of(row, j) for j in range(picks)]
            fields = jnp.concatenate(
                [jnp.concatenate([base[half, place] for place in places], axis=0) for half in range(2)],
                axis=1)
            product = jnp.dot(masses_of(row), fields, preferred_element_type=F32)
            weighted[pl.ds(pl.multiple_of(row * size, size), size), pl.ds(lanes_own, 2 * width)] = (
                product.astype(BF16))
        rows = pl.ds(pl.multiple_of(group * rim, rim), rim)
        add(0, 2, 0, 2, transposed_dot(near_fields(group + 1), weighted[rows, pl.ds(lanes_own, 2 * width)]))

    share_own(0, 0, 2)()
    fetch_eig.wait()

    def slot_of(order):
        return jnp.where(c == 1, order, pieces + 1 - order)

    def phase(index):
        lanes = lanes_far[index]
        known = 2 + index

        def rows_at(order):
            return pl.ds(pl.multiple_of((slot_of(order) - 1) * rim, rim), rim)

        def admit(order):
            first = pl.multiple_of(slot_of(order) * HB, HB)
            win[pl.ds(first, HB)] = far[index, pl.ds(first, HB)]

        def gathered(order, count):
            slot = slot_of(order)
            parts = [held(base, 0, slot), held(base, 1, slot)]
            return jnp.concatenate(parts + [held(far, i, slot) for i in range(count)], axis=1)

        def meet(order):
            rows = rows_at(order)
            parts = [weighted[rows, pl.ds(lanes_own, 2 * width)]]
            parts += [weighted[rows, pl.ds(lanes_far[i], width)] for i in range(index)]
            earlier = jnp.concatenate(parts, axis=1) if index else parts[0]
            add(known, known + 1, 0, known, transposed_dot(held(far, index, slot_of(order)), earlier))

        def project(order):
            vectors = jnp.concatenate(
                [eig[pl.ds(lanes_own, 2 * width)]] + [eig[pl.ds(lanes_far[i], width)] for i in range(2)],
                axis=0)
            modes[rows_at(order), :] = jnp.dot(gathered(order, 2), vectors,
                                               preferred_element_type=F32).astype(BF16)

        def work(order):
            slot = slot_of(order)
            for i in range(HB):
                row = (slot - 1) * HB + i
                fields = jnp.concatenate([win[place_of(row, j)] for j in range(picks)], axis=0)
                product = jnp.dot(masses_of(row), fields, preferred_element_type=F32)
                weighted[pl.ds(pl.multiple_of(row * size, size), size), pl.ds(lanes, width)] = (
                    product.astype(BF16))
            late[index, :, 0:(known + 1) * width] += transposed_dot(
                weighted[rows_at(order), pl.ds(lanes, width)], gathered(order, index + 1))

        wait_rim(far, index, recv_far.at[index, 1])
        mid = far.at[index, pl.ds(slot_of(1) * HB, HB)]
        forward = remote(mid, far.at[index, pl.ds(c * top, HB)], fwd_sems.at[index],
                         recv_far.at[index, 0], (s, partner))
        forward.start()
        admit(1)
        meet(1)
        if index == 1:
            project(1)
        wait_rim(far, index, recv_far.at[index, 0])
        admit(0)

        @pl.loop(0, pieces - 2)
        def _(p):
            wait_rim(far, index, recv_far.at[index, p + 2])
            admit(p + 2)
            meet(p + 2)
            if index == 1:
                project(p + 2)
            if index == 0:
                ready = p == pieces - 3

                @pl.when(ready & (c == 0))
                def _():
                    sent(2, 1)
                    pl.semaphore_signal(gate, inc=1, device_id=(s, partner), device_id_type=MESH)

                @pl.when(ready & (c == 1))
                def _():
                    pl.semaphore_wait(gate, 1)
                    pl.when(cross_rim)(cross.start)
                    for copy in mains:
                        copy.start()
                    cross_edge.start()
            work(p + 1)

        wait_rim(far, index, recv_far.at[index, pieces])
        if index == 1:
            send_far_band(0, known)
        admit(pieces)
        meet(pieces)
        finish = share_own(index + 1, known, known + 1)
        if index == 1:
            give_far(1, known, known + 1)
        work(pieces - 1)

        if index == 0:
            finish()
            pl.when(outer)(lambda: wait_rim(far, index, recv_far.at[index, pieces + 1]))
            admit(pieces + 1)
            work(pieces)
            for j in range(known + 1):
                acc[known, j * width:(j + 1) * width] = late[index, :, j * width:(j + 1) * width].T
            give_far(0, 0, known + 1)
            pack_far_band(0, 0, known + 1)
            forward.wait_send()
            return

        last_give = remote(late.at[index], given_late, give_sems.at[5], take_sems.at[5], (s, partner))

        @pl.when(jnp.logical_not(edge))
        def _():
            pl.when(outer)(lambda: wait_rim(far, index, recv_far.at[index, pieces + 1]))
            admit(pieces + 1)
            work(pieces)
            last_give.start()

        finish()
        pack_far_band(1, known, known + 1)
        send_far_band(known, known + 1)

        @pl.when(edge)
        def _():
            wait_rim(far, index, recv_far.at[index, pieces + 1])
            admit(pieces + 1)
            work(pieces)
            last_give.wait_recv()
            for t in range(n):
                column = jnp.where(z < n // 2, n - 1 - t, t)
                j = lax.rem(column, 2) + jnp.where(column // 2 == y, 0, 2)
                lanes_of = pl.ds(pl.multiple_of(j * width, width), width)
                value = (late[index, :, lanes_of] + given_late[:, lanes_of]).T
                tiles[2, t] = value.astype(BF16).reshape(tiles.shape[2:])
                for half in range(2):
                    remote(tiles.at[2, t, half], recv.at[ns + s], tile_sems.at[0], tile_sems.at[1],
                           (2 * column + half, 2 * yo + 1)).start()

        project(pieces)
        forward.wait_send()
        pl.when(jnp.logical_not(edge))(last_give.wait_send)

    phase(0)
    phase(1)

    pl.when(c == 0)(lambda: sent(2 * pieces - 2, 0))
    pl.when(c == 1)(lambda: sent(2 * pieces, 0))
    cross_edge.wait_send()
    own.wait_send()
    pl.when(jnp.logical_not(edge))(plane_edge.wait_send)
    pl.when(plane_rim)(plane.wait_send)
    pl.when(cross_rim)(cross.wait_send)
    tile_bytes = remote(recv.at[pl.ds(0, ns)], recv.at[pl.ds(0, ns)], tile_sems.at[0], tile_sems.at[1],
                        (s, partner))
    own_tiles = recv.at[pl.ds(0, ns - 1)]
    remote(own_tiles, own_tiles, tile_sems.at[0], tile_sems.at[1], (s, partner)).wait_send()

    @pl.when(c == 0)
    def _():
        for order, first, last in ((0, 0, n - 1), (1, n - 1, n)):
            give(1, order, 2, first, last).wait_send()

    pl.when(c == 1)(tile_bytes.wait_send)
    pl.when(edge)(tile_bytes.wait_send)
    all_tiles = recv.at[pl.ds(0, 2 * ns - 1)]
    remote(all_tiles, all_tiles, tile_sems.at[0], tile_sems.at[1], (s, partner)).wait_recv()
    total = recv[0].astype(F32)
    for i in range(1, 2 * ns):
        total = total + recv[i].astype(F32)
    corr_out[...] = total * scale


def deliver(weighted, modes, corr, weighted_out, modes_out, corr_out, sems):
    pairs = ((weighted, weighted_out), (modes, modes_out), (corr, corr_out))
    copies = [pltpu.make_async_copy(held, target, sems.at[i]) for i, (held, target) in enumerate(pairs)]
    for copy in copies:
        copy.start()
    for copy in copies:
        copy.wait()


def fast_shards(n, ns, snapshots, mass_blocks, neighbours, eigvecs):
    own_blocks, picks, size, _ = mass_blocks.shape
    total, width = snapshots.shape
    rows = total // n
    snaps = n * width
    pieces = own_blocks // HB
    sem = pltpu.SemaphoreType.DMA
    regular = pltpu.SemaphoreType.REGULAR
    vmem = pltpu.VMEM
    nz = ns // 2
    tile = snaps // ns
    held = own_blocks + 2 * HB
    modes_count = eigvecs.shape[1]
    hbm = pl.BlockSpec(memory_space=pltpu.HBM)
    inside = pl.BlockSpec(memory_space=pltpu.VMEM)
    block = (size, width)
    weighted, modes, corr = pl.pallas_call(
        functools.partial(fused, n, ns, 1.0 / (total * ns)),
        out_shape=(jax.ShapeDtypeStruct((rows, snaps), BF16),
                   jax.ShapeDtypeStruct((rows, modes_count), BF16),
                   jax.ShapeDtypeStruct((tile, width), F32)),
        in_specs=[hbm] * 4,
        out_specs=(inside, inside, inside),
        scratch_shapes=[
            vmem((2, held) + block, BF16), vmem((2, held) + block, BF16), vmem((held,) + block, BF16),
            vmem(mass_blocks.shape, BF16), vmem(eigvecs.shape, BF16),
            pltpu.SMEM((picks, own_blocks), jnp.int32), vmem((n, snaps, width), F32),
            vmem((2, width, snaps), F32), vmem((2, snaps, width), F32), vmem((width, snaps), F32),
            vmem((3, n, 2, tile, width), BF16), vmem((2 * ns, tile, width), BF16),
            sem((5,)), sem, sem, sem((2,)), sem((2,)), sem((2, pieces + 2)), sem((4,)), sem((2,)),
            sem((6,)), sem((6,)), sem((2,)), regular, regular((nz + 1,)),
        ],
        compiler_params=pltpu.CompilerParams(collective_id=0, has_side_effects=True,
                                             vmem_limit_bytes=40 * 2**20),
        name="fused",
    )(*(pltpu.with_memory_space_constraint(a, pltpu.HBM) for a in (
        neighbours.T, snapshots.reshape(total // size, size, width), mass_blocks, eigvecs)))
    weighted, modes, corr = pl.pallas_call(
        deliver,
        out_shape=tuple(pltpu.HBM(a.shape, a.dtype) for a in (weighted, modes, corr)),
        in_specs=[inside] * 3,
        out_specs=(hbm,) * 3,
        scratch_shapes=[sem((3,))],
        compiler_params=pltpu.CompilerParams(vmem_limit_bytes=2**20),
        name="deliver",
    )(*(pltpu.with_memory_space_constraint(a, pltpu.VMEM) for a in (weighted, modes, corr)))
    return weighted, corr.T, modes


def shifted(block, axis, distance):
    devices = range(lax.axis_size(axis))
    route = [(i - distance, i) for i in devices if i - distance in devices]
    return lax.ppermute(block, axis, route)


def plain_shards(snapshots, mass_blocks, neighbours, eigvecs):
    local_rows = lax.all_to_all(snapshots, "snap", split_axis=0, concat_axis=1, tiled=True)
    row_count, col_count = local_rows.shape
    block_size = mass_blocks.shape[2]
    rim_rows = HB * block_size
    below_rim = shifted(local_rows[row_count - rim_rows :], ("space", "snap"), 1)
    above_rim = shifted(local_rows[:rim_rows], ("space", "snap"), -1)
    extended = jnp.concatenate([below_rim, local_rows, above_rim], axis=0).reshape(
        -1, block_size, col_count
    )
    first_block = lax.axis_index(("space", "snap")) * (row_count // block_size)
    local_ids = neighbours - first_block + HB
    nearby = extended[local_ids]
    weighted = jnp.einsum("bjrc,bjcs->brs", mass_blocks, nearby, preferred_element_type=jnp.float32)
    weighted = weighted.reshape(row_count, col_count).astype(jnp.bfloat16)
    partial_corr = jnp.dot(weighted.T, local_rows, preferred_element_type=jnp.float32)
    band = lax.psum_scatter(partial_corr, "snap", scatter_dimension=0, tiled=True)
    correlation = lax.psum_scatter(band, "space", scatter_dimension=1, tiled=True)
    cell_total = row_count * lax.axis_size("space") * lax.axis_size("snap")
    correlation = correlation * (1.0 / cell_total)
    modes = jnp.dot(local_rows, eigvecs, preferred_element_type=jnp.float32).astype(jnp.bfloat16)
    return (weighted, correlation, modes)


def solution(mesh):
    n, ns = mesh.shape["snap"], mesh.shape["space"]

    def shards(snapshots, mass_blocks, neighbours, eigvecs):
        width = snapshots.shape[1]
        own_blocks, _, size, _ = mass_blocks.shape
        rows = own_blocks * size
        whole = n == 4 and ns == 2 * n and width % 128 == 0 and width == size
        if whole and snapshots.shape[0] == n * rows and own_blocks % HB == 0 and own_blocks >= 4 * HB:
            return fast_shards(n, ns, snapshots, mass_blocks, neighbours, eigvecs)
        return plain_shards(snapshots, mass_blocks, neighbours, eigvecs)

    in_specs = (
        P("space", "snap"),
        P(("space", "snap"), None, None, None),
        P(("space", "snap"), None),
        P(),
    )
    out_specs = (P(("space", "snap"), None), P("snap", "space"), P(("space", "snap"), None))
    return jax.shard_map(shards, mesh=mesh, in_specs=in_specs, out_specs=out_specs, check_vma=False)
```

```python
import functools

import jax
import jax.numpy as jnp
from jax import lax
from jax.experimental import pallas as pl
from jax.experimental.pallas import tpu as pltpu
from jax.sharding import PartitionSpec as P

HB = 4
MESH = pl.DeviceIdType.MESH
BF16 = jnp.bfloat16
F32 = jnp.float32


def transposed_dot(left, right):
    return lax.dot_general(left, right, (((0,), (0,)), ((), ())), preferred_element_type=F32)


def fused(n, ns, near_hbm, src, mass_hbm, eig_hbm, weighted, modes, recv,
          base, far, win, mass, eig, near, acc, late, given, given_late, tiles,
          loc, send_own, recv_own, recv_rim, send_far, recv_far, send_out, fwd_sems, give_sems, take_sems,
          tile_sems, gate, sync):
    nz = ns // 2
    s, k = lax.axis_index("space"), lax.axis_index("snap")
    y, c, z, x = k // 2, k % 2, s // 2, s % 2
    yo = 1 - y
    partner = 2 * y + 1 - c
    blocks, size, width = src.shape
    own_blocks = blocks // n
    chip_blocks = 2 * own_blocks
    pieces = own_blocks // HB
    rim = HB * size
    picks = mass.shape[1]
    top = HB + own_blocks
    first_block = (s * n + k) * own_blocks - HB
    lanes_own = pl.multiple_of(2 * y * width, 2 * width)
    lanes_far = [pl.multiple_of((2 * yo + i) * width, width) for i in range(2)]

    def local(i, origin, target):
        return pltpu.make_async_copy(origin, target, loc.at[i])

    def remote(origin, target, sends, recvs, device):
        return pltpu.make_async_remote_copy(src_ref=origin, dst_ref=target, send_sem=sends,
                                            recv_sem=recvs, device_id=device, device_id_type=MESH)

    def rows_of(first, count):
        return src.at[pl.ds(first, count)]

    def hail(sem):
        for t in range(1, n):
            pl.semaphore_signal(sem, inc=1, device_id=(s, lax.rem(k + t, n)), device_id_type=MESH)
        pl.semaphore_signal(sem, inc=1, device_id=(2 * z + 1 - x, k), device_id_type=MESH)

        @pl.when(z > 0)
        def _():
            pl.semaphore_signal(sem, inc=1, device_id=(s - 2, k), device_id_type=MESH)

        @pl.when(z < nz - 1)
        def _():
            pl.semaphore_signal(sem, inc=1, device_id=(s + 2, k), device_id_type=MESH)

    def heed(sem):
        pl.semaphore_wait(sem, n + jnp.where(z > 0, 1, 0) + jnp.where(z < nz - 1, 1, 0))

    barrier = pltpu.get_barrier_semaphore()
    hail(barrier)
    edge = c != y
    cross_halo = jnp.logical_not(edge) & (((y == 0) & (s > 0)) | ((y == 1) & (s < ns - 1)))
    outer = edge | cross_halo
    cross_rim = ((y == 0) & (s > 0)) | ((y == 1) & (s < ns - 1))
    plane_rim = ((y == 0) & (s < ns - 1)) | ((y == 1) & (s > 0))

    keep = local(0, rows_of(y * chip_blocks + c * (own_blocks - HB), own_blocks + HB),
                 base.at[c, pl.ds((1 - c) * HB, own_blocks + HB)])
    edge_rows = rows_of(chip_blocks - y * HB, HB)
    edge_keep = local(1, edge_rows, base.at[c, pl.ds(yo * top, HB)])
    fetch = local(2, mass_hbm, mass)
    fetch_eig = local(3, eig_hbm, eig)
    fetch_near = local(4, near_hbm, near)

    def main_copy(o, co):
        at = yo * chip_blocks + jnp.where(co == 0, (pieces - 1 - o) * HB, own_blocks + o * HB)
        to = jnp.where(co == 0, (pieces - o) * HB, (1 + o) * HB)
        watched = jnp.where(c == 0, 1, 0) if o == pieces - 4 else 0
        return remote(rows_of(at, HB), far.at[c, pl.ds(to, HB)], send_far.at[watched],
                      recv_far.at[c, o + 1], (s, 2 * yo + co))

    mains = [main_copy(0, yo)]
    for o in range(1, pieces):
        mains += [main_copy(o, yo), main_copy(o - 1, y)]
    mains.append(main_copy(pieces - 1, y))

    def sent(count, i):
        rows = rows_of(0, count * HB)
        remote(rows, rows, send_far.at[i], recv_own, (s, partner)).wait_send()

    half_rim = HB // 2
    edge_first = yo * half_rim
    cross_edges = [
        remote(rows_of(chip_blocks - yo * HB + at, half_rim), far.at[c, pl.ds(y * top + at, half_rim)],
               send_out.at[4 * i], recv_far.at[c, pieces + 1 + i], (s, 2 * yo + y))
        for i, at in enumerate((edge_first, half_rim - edge_first))]
    cross = remote(rows_of(y * (blocks - HB), HB), far.at[c, pl.ds(yo * top, HB)],
                   send_out.at[1], recv_far.at[c, pieces + 1], (s + 2 * y - 1, yo * (n - 1)))
    plane = remote(rows_of(yo * (blocks - HB), HB), base.at[c, pl.ds(y * top, HB)],
                   send_out.at[2], recv_rim.at[c], (s + 1 - 2 * y, y * (n - 1)))
    plane_edge = remote(edge_rows, base.at[c, pl.ds(yo * top, HB)], send_out.at[3], recv_rim.at[c],
                        (s, partner))
    own = remote(rows_of(y * chip_blocks + (1 - c) * (own_blocks - HB), own_blocks + HB),
                 base.at[c, pl.ds(c * HB, own_blocks + HB)], send_own, recv_own, (s, partner))

    keep.start()
    pl.when(edge)(edge_keep.start)
    fetch_near.start()
    fetch.start()
    fetch_eig.start()

    acc[...] = jnp.zeros_like(acc)
    late[...] = jnp.zeros_like(late)
    heed(barrier)

    @pl.when(c == 0)
    def _():
        for copy in mains:
            copy.start()
        for copy in cross_edges:
            copy.start()

    own.start()
    pl.when(jnp.logical_not(edge))(plane_edge.start)
    for i in range(nz + 1):
        hail(sync.at[i])
        heed(sync.at[i])
    pl.when(plane_rim)(plane.start)
    pl.when(cross_rim & (c == 0))(cross.start)

    def wait_rim(buffer, index, recvs, count=HB):
        rows = buffer.at[index, pl.ds(0, count)]
        remote(rows, rows, send_own, recvs, (s, partner)).wait_recv()

    def masses_of(row):
        return jnp.concatenate([mass[row, j] for j in range(picks)], axis=1)

    def place_of(row, j):
        return jnp.clip(near[j, row] - first_block, 0, base.shape[1] - 1)

    def span(first, last):
        return pl.ds(first * width, (last - first) * width)

    def give(kind, order, band, first, last):
        rows = span(first, last)
        return remote(acc.at[band, rows], given.at[kind, rows], give_sems.at[3 * kind + order],
                      take_sems.at[3 * kind + order], (s, partner))

    def column_of(j):
        return 2 * y + j if j < 2 else 2 * yo + j - 2

    def pack(kind, j, value):
        tiles[kind, j] = value.astype(BF16).reshape(tiles.shape[2:])

    def send_tiles(kind, j, slot, band):
        for half in range(2):
            target = 2 * column_of(j) + half
            copy = remote(tiles.at[kind, j, half], recv.at[slot], tile_sems.at[0], tile_sems.at[1],
                          (target, band))
            if kind:
                copy.start()
                continue
            mine = target == s
            pl.when(jnp.logical_not(mine))(copy.start)

            @pl.when(mine)
            def _():
                recv[slot] = tiles[kind, j, half]

    def share_own(order, first, last):
        copy = give(0, order, 1 - c, first, last)
        copy.start()

        def finish():
            copy.wait()
            for j in range(first, last):
                rows = span(j, j + 1)
                pack(0, j, acc[c, rows] + given[0, rows])
                send_tiles(0, j, s, k)

        return finish

    def give_far(order, first, last):
        @pl.when(c == 0)
        def _():
            give(1, order, 2, first, last).start()

    def pack_far_band(order, first, last):
        @pl.when(c == 1)
        def _():
            give(1, order, 2, first, last).wait_recv()
            for j in range(first, last):
                rows = span(j, j + 1)
                pack(1, j, acc[2, rows] + given[1, rows])

    def send_far_band(first, last):
        @pl.when(c == 1)
        def _():
            for j in range(first, last):
                send_tiles(1, j, ns + s, 2 * yo)

    keep.wait()
    own.wait_recv()
    pl.when(edge)(edge_keep.wait)
    for i in range(2):
        @pl.when(outer & (jnp.logical_not(edge) | (c != i)))
        def _():
            wait_rim(base, i, recv_rim.at[i])
    fetch.wait()
    fetch_near.wait()

    def held(buffer, index, slot, first=0, count=HB):
        return buffer[index, pl.ds(slot * HB + first, count)].reshape(count * size, width)

    def add(first, last, band, count, value):
        for i in range(count):
            acc[band + i, first * width:last * width] += value[:, i * width:(i + 1) * width]

    def near_fields(slot):
        return jnp.concatenate([held(base, 0, slot), held(base, 1, slot)], axis=1)

    @pl.loop(0, pieces)
    def _(group):
        for i in range(HB):
            row = group * HB + i
            places = [place_of(row, j) for j in range(picks)]
            fields = jnp.concatenate(
                [jnp.concatenate([base[half, place] for place in places], axis=0) for half in range(2)],
                axis=1)
            product = jnp.dot(masses_of(row), fields, preferred_element_type=F32)
            weighted[pl.ds(pl.multiple_of(row * size, size), size), pl.ds(lanes_own, 2 * width)] = (
                product.astype(BF16))
        rows = pl.ds(pl.multiple_of(group * rim, rim), rim)
        add(0, 2, 0, 2, transposed_dot(near_fields(group + 1), weighted[rows, pl.ds(lanes_own, 2 * width)]))

    share_own(0, 0, 2)()
    fetch_eig.wait()

    def slot_of(order):
        return jnp.where(c == 1, order, pieces + 1 - order)

    def phase(index):
        lanes = lanes_far[index]
        known = 2 + index

        def rows_at(order, first=0, count=HB):
            at = (slot_of(order) - 1) * rim + first * size
            return pl.ds(pl.multiple_of(at, size), count * size)

        def admit(order, first=0, count=HB):
            at = slot_of(order) * HB + first
            win[pl.ds(at, count)] = far[index, pl.ds(at, count)]

        def gathered(order, count, first=0, rows=HB):
            slot = slot_of(order)
            parts = [held(base, i, slot, first, rows) for i in range(2)]
            return jnp.concatenate(parts + [held(far, i, slot, first, rows) for i in range(count)], axis=1)

        def meet(order):
            rows = rows_at(order)
            parts = [weighted[rows, pl.ds(lanes_own, 2 * width)]]
            parts += [weighted[rows, pl.ds(lanes_far[i], width)] for i in range(index)]
            earlier = jnp.concatenate(parts, axis=1) if index else parts[0]
            add(known, known + 1, 0, known, transposed_dot(held(far, index, slot_of(order)), earlier))

        def project(order):
            vectors = jnp.concatenate(
                [eig[pl.ds(lanes_own, 2 * width)]] + [eig[pl.ds(lanes_far[i], width)] for i in range(2)],
                axis=0)
            modes[rows_at(order), :] = jnp.dot(gathered(order, 2), vectors,
                                               preferred_element_type=F32).astype(BF16)

        def work(order, first=0, count=HB):
            for i in range(count):
                row = (slot_of(order) - 1) * HB + first + i
                fields = jnp.concatenate([win[place_of(row, j)] for j in range(picks)], axis=0)
                product = jnp.dot(masses_of(row), fields, preferred_element_type=F32)
                weighted[pl.ds(pl.multiple_of(row * size, size), size), pl.ds(lanes, width)] = (
                    product.astype(BF16))
            late[index, :, 0:(known + 1) * width] += transposed_dot(
                weighted[rows_at(order, first, count), pl.ds(lanes, width)],
                gathered(order, index + 1, first, count))

        def wait_outer():
            @pl.when(edge)
            def _():
                for i in range(2):
                    wait_rim(far, index, recv_far.at[index, pieces + 1 + i], half_rim)

            @pl.when(cross_halo)
            def _():
                wait_rim(far, index, recv_far.at[index, pieces + 1])

        wait_rim(far, index, recv_far.at[index, 1])
        mid = far.at[index, pl.ds(slot_of(1) * HB, HB)]
        forward = remote(mid, far.at[index, pl.ds(c * top, HB)], fwd_sems.at[index],
                         recv_far.at[index, 0], (s, partner))
        forward.start()
        admit(1)
        meet(1)
        if index == 1:
            project(1)
        wait_rim(far, index, recv_far.at[index, 0])
        admit(0)

        @pl.loop(0, pieces - 2)
        def _(p):
            wait_rim(far, index, recv_far.at[index, p + 2])
            admit(p + 2)
            meet(p + 2)
            if index == 1:
                project(p + 2)
            if index == 0:
                ready = p == pieces - 3

                @pl.when(ready & (c == 0))
                def _():
                    sent(2, 1)
                    pl.semaphore_signal(gate, inc=1, device_id=(s, partner), device_id_type=MESH)

                @pl.when(ready & (c == 1))
                def _():
                    pl.semaphore_wait(gate, 1)
                    pl.when(cross_rim)(cross.start)
                    for copy in mains:
                        copy.start()
                    for copy in cross_edges:
                        copy.start()
            work(p + 1)

        wait_rim(far, index, recv_far.at[index, pieces])
        if index == 1:
            send_far_band(0, known)
        admit(pieces)
        meet(pieces)
        finish = share_own(index + 1, known, known + 1)
        if index == 1:
            give_far(1, known, known + 1)
        work(pieces - 1)

        if index == 0:
            finish()
            wait_outer()
            admit(pieces + 1)
            work(pieces)
            for j in range(known + 1):
                acc[known, j * width:(j + 1) * width] = late[index, :, j * width:(j + 1) * width].T
            give_far(0, 0, known + 1)
            pack_far_band(0, 0, known + 1)
            forward.wait_send()
            return

        last_give = remote(late.at[index], given_late, give_sems.at[5], take_sems.at[5], (s, partner))

        @pl.when(jnp.logical_not(edge))
        def _():
            pl.when(cross_halo)(lambda: wait_rim(far, index, recv_far.at[index, pieces + 1]))
            admit(pieces + 1)
            work(pieces)
            last_give.start()

        @pl.when(edge)
        def _():
            for i, at in enumerate((y * half_rim, yo * half_rim)):
                wait_rim(far, index, recv_far.at[index, pieces + 1 + i], half_rim)
                admit(pieces + 1, at, half_rim)
                work(pieces, at, half_rim)
            last_give.wait_recv()
            for t in range(n):
                column = jnp.where(z < n // 2, n - 1 - t, t)
                j = lax.rem(column, 2) + jnp.where(column // 2 == y, 0, 2)
                lanes_of = pl.ds(pl.multiple_of(j * width, width), width)
                value = (late[index, :, lanes_of] + given_late[:, lanes_of]).astype(BF16)
                tiles[2, t] = value.T.reshape(tiles.shape[2:])
                for half in range(2):
                    remote(tiles.at[2, t, half], recv.at[ns + s], tile_sems.at[0], tile_sems.at[1],
                           (2 * column + half, 2 * yo + 1)).start()

        finish()
        pack_far_band(1, known, known + 1)
        send_far_band(known, known + 1)
        project(pieces)
        forward.wait_send()
        pl.when(jnp.logical_not(edge))(last_give.wait_send)

    phase(0)
    phase(1)

    pl.when(c == 0)(lambda: sent(2 * pieces - 2, 0))
    pl.when(c == 1)(lambda: sent(2 * pieces, 0))
    for copy in cross_edges:
        copy.wait_send()
    own.wait_send()
    pl.when(jnp.logical_not(edge))(plane_edge.wait_send)
    pl.when(plane_rim)(plane.wait_send)
    pl.when(cross_rim)(cross.wait_send)
    tile_bytes = remote(recv.at[pl.ds(0, ns)], recv.at[pl.ds(0, ns)], tile_sems.at[0], tile_sems.at[1],
                        (s, partner))
    own_tiles = recv.at[pl.ds(0, ns - 1)]
    remote(own_tiles, own_tiles, tile_sems.at[0], tile_sems.at[1], (s, partner)).wait_send()

    @pl.when(c == 0)
    def _():
        for order, first, last in ((0, 0, n - 1), (1, n - 1, n)):
            give(1, order, 2, first, last).wait_send()

    pl.when(c == 1)(tile_bytes.wait_send)
    pl.when(edge)(tile_bytes.wait_send)
    all_tiles = recv.at[pl.ds(0, 2 * ns - 1)]
    remote(all_tiles, all_tiles, tile_sems.at[0], tile_sems.at[1], (s, partner)).wait_recv()


def deliver(scale, weighted, modes, parts, weighted_out, modes_out, corr_out, corr, sems):
    pairs = ((weighted, weighted_out), (modes, modes_out), (corr, corr_out))
    copies = [pltpu.make_async_copy(held, target, sems.at[i]) for i, (held, target) in enumerate(pairs)]
    for copy in copies[:2]:
        copy.start()
    total = parts[0].astype(F32)
    for i in range(1, parts.shape[0]):
        total = total + parts[i].astype(F32)
    corr[...] = total * scale
    copies[2].start()
    for copy in copies:
        copy.wait()


def fast_shards(n, ns, snapshots, mass_blocks, neighbours, eigvecs):
    own_blocks, picks, size, _ = mass_blocks.shape
    total, width = snapshots.shape
    rows = total // n
    snaps = n * width
    pieces = own_blocks // HB
    sem = pltpu.SemaphoreType.DMA
    regular = pltpu.SemaphoreType.REGULAR
    vmem = pltpu.VMEM
    nz = ns // 2
    tile = snaps // ns
    held = own_blocks + 2 * HB
    modes_count = eigvecs.shape[1]
    hbm = pl.BlockSpec(memory_space=pltpu.HBM)
    inside = pl.BlockSpec(memory_space=pltpu.VMEM)
    block = (size, width)
    weighted, modes, parts = pl.pallas_call(
        functools.partial(fused, n, ns),
        out_shape=(jax.ShapeDtypeStruct((rows, snaps), BF16),
                   jax.ShapeDtypeStruct((rows, modes_count), BF16),
                   jax.ShapeDtypeStruct((2 * ns, tile, width), BF16)),
        in_specs=[hbm] * 4,
        out_specs=(inside, inside, inside),
        scratch_shapes=[
            vmem((2, held) + block, BF16), vmem((2, held) + block, BF16), vmem((held,) + block, BF16),
            vmem(mass_blocks.shape, BF16), vmem(eigvecs.shape, BF16),
            pltpu.SMEM((picks, own_blocks), jnp.int32), vmem((n, snaps, width), F32),
            vmem((2, width, snaps), F32), vmem((2, snaps, width), F32), vmem((width, snaps), F32),
            vmem((3, n, 2, tile, width), BF16),
            sem((5,)), sem, sem, sem((2,)), sem((2,)), sem((2, pieces + 3)), sem((5,)), sem((2,)),
            sem((6,)), sem((6,)), sem((2,)), regular, regular((nz + 1,)),
        ],
        compiler_params=pltpu.CompilerParams(collective_id=0, has_side_effects=True,
                                             vmem_limit_bytes=40 * 2**20),
        name="fused",
    )(*(pltpu.with_memory_space_constraint(a, pltpu.HBM) for a in (
        neighbours.T, snapshots.reshape(total // size, size, width), mass_blocks, eigvecs)))
    weighted, modes, corr = pl.pallas_call(
        functools.partial(deliver, 1.0 / (total * ns)),
        out_shape=(pltpu.HBM(weighted.shape, BF16), pltpu.HBM(modes.shape, BF16), pltpu.HBM((tile, width), F32)),
        in_specs=[inside] * 3,
        out_specs=(hbm,) * 3,
        scratch_shapes=[vmem((tile, width), F32), sem((3,))],
        compiler_params=pltpu.CompilerParams(vmem_limit_bytes=2**20),
        name="deliver",
    )(*(pltpu.with_memory_space_constraint(a, pltpu.VMEM) for a in (weighted, modes, parts)))
    return weighted, corr.T, modes


def shifted(block, axis, distance):
    devices = range(lax.axis_size(axis))
    route = [(i - distance, i) for i in devices if i - distance in devices]
    return lax.ppermute(block, axis, route)


def plain_shards(snapshots, mass_blocks, neighbours, eigvecs):
    local_rows = lax.all_to_all(snapshots, "snap", split_axis=0, concat_axis=1, tiled=True)
    row_count, col_count = local_rows.shape
    block_size = mass_blocks.shape[2]
    rim_rows = HB * block_size
    below_rim = shifted(local_rows[row_count - rim_rows :], ("space", "snap"), 1)
    above_rim = shifted(local_rows[:rim_rows], ("space", "snap"), -1)
    extended = jnp.concatenate([below_rim, local_rows, above_rim], axis=0).reshape(
        -1, block_size, col_count
    )
    first_block = lax.axis_index(("space", "snap")) * (row_count // block_size)
    local_ids = neighbours - first_block + HB
    nearby = extended[local_ids]
    weighted = jnp.einsum("bjrc,bjcs->brs", mass_blocks, nearby, preferred_element_type=jnp.float32)
    weighted = weighted.reshape(row_count, col_count).astype(jnp.bfloat16)
    partial_corr = jnp.dot(weighted.T, local_rows, preferred_element_type=jnp.float32)
    band = lax.psum_scatter(partial_corr, "snap", scatter_dimension=0, tiled=True)
    correlation = lax.psum_scatter(band, "space", scatter_dimension=1, tiled=True)
    cell_total = row_count * lax.axis_size("space") * lax.axis_size("snap")
    correlation = correlation * (1.0 / cell_total)
    modes = jnp.dot(local_rows, eigvecs, preferred_element_type=jnp.float32).astype(jnp.bfloat16)
    return (weighted, correlation, modes)


def solution(mesh):
    n, ns = mesh.shape["snap"], mesh.shape["space"]

    def shards(snapshots, mass_blocks, neighbours, eigvecs):
        width = snapshots.shape[1]
        own_blocks, _, size, _ = mass_blocks.shape
        rows = own_blocks * size
        whole = n == 4 and ns == 2 * n and width % 128 == 0 and width == size
        if whole and snapshots.shape[0] == n * rows and own_blocks % HB == 0 and own_blocks >= 4 * HB:
            return fast_shards(n, ns, snapshots, mass_blocks, neighbours, eigvecs)
        return plain_shards(snapshots, mass_blocks, neighbours, eigvecs)

    in_specs = (
        P("space", "snap"),
        P(("space", "snap"), None, None, None),
        P(("space", "snap"), None),
        P(),
    )
    out_specs = (P(("space", "snap"), None), P("snap", "space"), P(("space", "snap"), None))
    return jax.shard_map(shards, mesh=mesh, in_specs=in_specs, out_specs=out_specs, check_vma=False)
```

```python
import functools

import jax
import jax.numpy as jnp
from jax import lax
from jax.experimental import pallas as pl
from jax.experimental.pallas import tpu as pltpu
from jax.sharding import PartitionSpec as P

HB = 4
MESH = pl.DeviceIdType.MESH
BF16 = jnp.bfloat16
F32 = jnp.float32


def transposed_dot(left, right):
    return lax.dot_general(left, right, (((0,), (0,)), ((), ())), preferred_element_type=F32)


def fused(n, ns, near_hbm, src, mass_hbm, eig_hbm, weighted, modes, recv,
          base, far, win, mass, eig, near, acc, late, given, given_late, tiles,
          loc, send_own, recv_own, recv_rim, send_far, recv_far, send_out, fwd_sems, give_sems, take_sems,
          tile_sems, gate, sync):
    nz = ns // 2
    s, k = lax.axis_index("space"), lax.axis_index("snap")
    y, c, z, x = k // 2, k % 2, s // 2, s % 2
    yo = 1 - y
    partner = 2 * y + 1 - c
    blocks, size, width = src.shape
    own_blocks = blocks // n
    chip_blocks = 2 * own_blocks
    pieces = own_blocks // HB
    rim = HB * size
    picks = mass.shape[1]
    top = HB + own_blocks
    first_block = (s * n + k) * own_blocks - HB
    lanes_own = pl.multiple_of(2 * y * width, 2 * width)
    lanes_far = [pl.multiple_of((2 * yo + i) * width, width) for i in range(2)]

    def local(i, origin, target):
        return pltpu.make_async_copy(origin, target, loc.at[i])

    def remote(origin, target, sends, recvs, device):
        return pltpu.make_async_remote_copy(src_ref=origin, dst_ref=target, send_sem=sends,
                                            recv_sem=recvs, device_id=device, device_id_type=MESH)

    def rows_of(first, count):
        return src.at[pl.ds(first, count)]

    def hail(sem):
        for t in range(1, n):
            pl.semaphore_signal(sem, inc=1, device_id=(s, lax.rem(k + t, n)), device_id_type=MESH)
        pl.semaphore_signal(sem, inc=1, device_id=(2 * z + 1 - x, k), device_id_type=MESH)

        @pl.when(z > 0)
        def _():
            pl.semaphore_signal(sem, inc=1, device_id=(s - 2, k), device_id_type=MESH)

        @pl.when(z < nz - 1)
        def _():
            pl.semaphore_signal(sem, inc=1, device_id=(s + 2, k), device_id_type=MESH)

    def heed(sem):
        pl.semaphore_wait(sem, n + jnp.where(z > 0, 1, 0) + jnp.where(z < nz - 1, 1, 0))

    barrier = pltpu.get_barrier_semaphore()
    hail(barrier)
    edge = c != y
    cross_halo = jnp.logical_not(edge) & (((y == 0) & (s > 0)) | ((y == 1) & (s < ns - 1)))
    outer = edge | cross_halo
    cross_rim = ((y == 0) & (s > 0)) | ((y == 1) & (s < ns - 1))
    plane_rim = ((y == 0) & (s < ns - 1)) | ((y == 1) & (s > 0))

    keep = local(0, rows_of(y * chip_blocks + c * (own_blocks - HB), own_blocks + HB),
                 base.at[c, pl.ds((1 - c) * HB, own_blocks + HB)])
    edge_rows = rows_of(chip_blocks - y * HB, HB)
    edge_keep = local(1, edge_rows, base.at[c, pl.ds(yo * top, HB)])
    fetch = local(2, mass_hbm, mass)
    fetch_eig = local(3, eig_hbm, eig)
    fetch_near = local(4, near_hbm, near)

    def main_copy(o, co):
        at = yo * chip_blocks + jnp.where(co == 0, (pieces - 1 - o) * HB, own_blocks + o * HB)
        to = jnp.where(co == 0, (pieces - o) * HB, (1 + o) * HB)
        watched = jnp.where(c == 0, 1, 0) if o == pieces - 4 else 0
        return remote(rows_of(at, HB), far.at[c, pl.ds(to, HB)], send_far.at[watched],
                      recv_far.at[c, o + 1], (s, 2 * yo + co))

    mains = [main_copy(0, yo)]
    for o in range(1, pieces):
        mains += [main_copy(o, yo), main_copy(o - 1, y)]
    mains.append(main_copy(pieces - 1, y))

    def sent(count, i):
        rows = rows_of(0, count * HB)
        remote(rows, rows, send_far.at[i], recv_own, (s, partner)).wait_send()

    half_rim = HB // 2
    edge_first = yo * half_rim
    cross_edges = [
        remote(rows_of(chip_blocks - yo * HB + at, half_rim), far.at[c, pl.ds(y * top + at, half_rim)],
               send_far.at[0], recv_far.at[c, pieces + 1 + i], (s, 2 * yo + y))
        for i, at in enumerate((edge_first, half_rim - edge_first))]
    cross = remote(rows_of(y * (blocks - HB), HB), far.at[c, pl.ds(yo * top, HB)],
                   send_out.at[0], recv_far.at[c, pieces + 1], (s + 2 * y - 1, yo * (n - 1)))
    plane = remote(rows_of(yo * (blocks - HB), HB), base.at[c, pl.ds(y * top, HB)],
                   send_out.at[1], recv_rim.at[c], (s + 1 - 2 * y, y * (n - 1)))
    plane_edge = remote(edge_rows, base.at[c, pl.ds(yo * top, HB)], send_out.at[2], recv_rim.at[c],
                        (s, partner))
    own = remote(rows_of(y * chip_blocks + (1 - c) * (own_blocks - HB), own_blocks + HB),
                 base.at[c, pl.ds(c * HB, own_blocks + HB)], send_own, recv_own, (s, partner))

    keep.start()
    pl.when(edge)(edge_keep.start)
    fetch_near.start()
    fetch.start()
    fetch_eig.start()

    acc[...] = jnp.zeros_like(acc)
    late[...] = jnp.zeros_like(late)
    heed(barrier)

    @pl.when(c == 0)
    def _():
        for copy in mains:
            copy.start()
        for copy in cross_edges:
            copy.start()

    own.start()
    pl.when(jnp.logical_not(edge))(plane_edge.start)
    for i in range(nz):
        hail(sync.at[i])
        heed(sync.at[i])
    pl.when(plane_rim)(plane.start)
    pl.when(cross_rim & (c == 0))(cross.start)

    def wait_rim(buffer, index, recvs, count=HB):
        rows = buffer.at[index, pl.ds(0, count)]
        remote(rows, rows, send_own, recvs, (s, partner)).wait_recv()

    def masses_of(row):
        return jnp.concatenate([mass[row, j] for j in range(picks)], axis=1)

    def place_of(row, j):
        return jnp.clip(near[j, row] - first_block, 0, base.shape[1] - 1)

    def span(first, last):
        return pl.ds(first * width, (last - first) * width)

    def give(kind, order, band, first, last):
        rows = span(first, last)
        return remote(acc.at[band, rows], given.at[kind, rows], give_sems.at[3 * kind + order],
                      take_sems.at[3 * kind + order], (s, partner))

    def column_of(j):
        return 2 * y + j if j < 2 else 2 * yo + j - 2

    def pack(kind, j, value):
        tiles[kind, j] = value.astype(BF16).reshape(tiles.shape[2:])

    def send_tiles(kind, j, slot, band):
        for half in range(2):
            target = 2 * column_of(j) + half
            copy = remote(tiles.at[kind, j, half], recv.at[slot], tile_sems.at[0], tile_sems.at[1],
                          (target, band))
            if kind:
                copy.start()
                continue
            mine = target == s
            pl.when(jnp.logical_not(mine))(copy.start)

            @pl.when(mine)
            def _():
                recv[slot] = tiles[kind, j, half]

    def share_own(order, first, last):
        copy = give(0, order, 1 - c, first, last)
        copy.start()

        def finish():
            copy.wait()
            for j in range(first, last):
                rows = span(j, j + 1)
                pack(0, j, acc[c, rows] + given[0, rows])
                send_tiles(0, j, s, k)

        return finish

    def give_far(order, first, last):
        @pl.when(c == 0)
        def _():
            give(1, order, 2, first, last).start()

    def pack_far_band(order, first, last):
        @pl.when(c == 1)
        def _():
            give(1, order, 2, first, last).wait_recv()
            for j in range(first, last):
                rows = span(j, j + 1)
                pack(1, j, acc[2, rows] + given[1, rows])

    def send_far_band(first, last):
        @pl.when(c == 1)
        def _():
            for j in range(first, last):
                send_tiles(1, j, ns + s, 2 * yo)

    keep.wait()
    own.wait_recv()
    pl.when(edge)(edge_keep.wait)
    for i in range(2):
        @pl.when(outer & (jnp.logical_not(edge) | (c != i)))
        def _():
            wait_rim(base, i, recv_rim.at[i])
    fetch.wait()
    fetch_near.wait()

    def held(buffer, index, slot, first=0, count=HB):
        return buffer[index, pl.ds(slot * HB + first, count)].reshape(count * size, width)

    def add(first, last, band, count, value):
        for i in range(count):
            acc[band + i, first * width:last * width] += value[:, i * width:(i + 1) * width]

    def near_fields(slot):
        return jnp.concatenate([held(base, 0, slot), held(base, 1, slot)], axis=1)

    @pl.loop(0, pieces)
    def _(group):
        for i in range(HB):
            row = group * HB + i
            places = [place_of(row, j) for j in range(picks)]
            fields = jnp.concatenate(
                [jnp.concatenate([base[half, place] for place in places], axis=0) for half in range(2)],
                axis=1)
            product = jnp.dot(masses_of(row), fields, preferred_element_type=F32)
            weighted[pl.ds(pl.multiple_of(row * size, size), size), pl.ds(lanes_own, 2 * width)] = (
                product.astype(BF16))
        rows = pl.ds(pl.multiple_of(group * rim, rim), rim)
        add(0, 2, 0, 2, transposed_dot(near_fields(group + 1), weighted[rows, pl.ds(lanes_own, 2 * width)]))

    share_own(0, 0, 2)()
    fetch_eig.wait()

    def slot_of(order):
        return jnp.where(c == 1, order, pieces + 1 - order)

    def phase(index):
        lanes = lanes_far[index]
        known = 2 + index

        def rows_at(order, first=0, count=HB):
            at = (slot_of(order) - 1) * rim + first * size
            return pl.ds(pl.multiple_of(at, size), count * size)

        def admit(order, first=0, count=HB):
            at = slot_of(order) * HB + first
            win[pl.ds(at, count)] = far[index, pl.ds(at, count)]

        def gathered(order, count, first=0, rows=HB):
            slot = slot_of(order)
            parts = [held(base, i, slot, first, rows) for i in range(2)]
            return jnp.concatenate(parts + [held(far, i, slot, first, rows) for i in range(count)], axis=1)

        def meet(order):
            rows = rows_at(order)
            parts = [weighted[rows, pl.ds(lanes_own, 2 * width)]]
            parts += [weighted[rows, pl.ds(lanes_far[i], width)] for i in range(index)]
            earlier = jnp.concatenate(parts, axis=1) if index else parts[0]
            add(known, known + 1, 0, known, transposed_dot(held(far, index, slot_of(order)), earlier))

        def project(order):
            vectors = jnp.concatenate(
                [eig[pl.ds(lanes_own, 2 * width)]] + [eig[pl.ds(lanes_far[i], width)] for i in range(2)],
                axis=0)
            modes[rows_at(order), :] = jnp.dot(gathered(order, 2), vectors,
                                               preferred_element_type=F32).astype(BF16)

        def work(order, first=0, count=HB):
            for i in range(count):
                row = (slot_of(order) - 1) * HB + first + i
                fields = jnp.concatenate([win[place_of(row, j)] for j in range(picks)], axis=0)
                product = jnp.dot(masses_of(row), fields, preferred_element_type=F32)
                weighted[pl.ds(pl.multiple_of(row * size, size), size), pl.ds(lanes, width)] = (
                    product.astype(BF16))
            late[index, :, 0:(known + 1) * width] += transposed_dot(
                weighted[rows_at(order, first, count), pl.ds(lanes, width)],
                gathered(order, index + 1, first, count))

        def wait_outer():
            @pl.when(edge)
            def _():
                for i in range(2):
                    wait_rim(far, index, recv_far.at[index, pieces + 1 + i], half_rim)

            @pl.when(cross_halo)
            def _():
                wait_rim(far, index, recv_far.at[index, pieces + 1])

        wait_rim(far, index, recv_far.at[index, 1])
        mid = far.at[index, pl.ds(slot_of(1) * HB, HB)]
        forward = remote(mid, far.at[index, pl.ds(c * top, HB)], fwd_sems.at[index],
                         recv_far.at[index, 0], (s, partner))
        forward.start()
        admit(1)
        meet(1)
        if index == 1:
            project(1)
        wait_rim(far, index, recv_far.at[index, 0])
        admit(0)

        @pl.loop(0, pieces - 2)
        def _(p):
            wait_rim(far, index, recv_far.at[index, p + 2])
            admit(p + 2)
            meet(p + 2)
            if index == 1:
                project(p + 2)
            if index == 0:
                ready = p == pieces - 3

                @pl.when(ready & (c == 0))
                def _():
                    sent(2, 1)
                    pl.semaphore_signal(gate, inc=1, device_id=(s, partner), device_id_type=MESH)

                @pl.when(ready & (c == 1))
                def _():
                    pl.semaphore_wait(gate, 1)
                    pl.when(cross_rim)(cross.start)
                    for copy in mains:
                        copy.start()
                    for copy in cross_edges:
                        copy.start()
            work(p + 1)

        wait_rim(far, index, recv_far.at[index, pieces])
        if index == 1:
            send_far_band(0, known)
        admit(pieces)
        meet(pieces)
        finish = share_own(index + 1, known, known + 1)
        if index == 1:
            give_far(1, known, known + 1)
        work(pieces - 1)

        if index == 0:
            finish()
            wait_outer()
            admit(pieces + 1)
            work(pieces)
            for j in range(known + 1):
                acc[known, j * width:(j + 1) * width] = late[index, :, j * width:(j + 1) * width].T
            give_far(0, 0, known + 1)
            pack_far_band(0, 0, known + 1)
            forward.wait_send()
            return

        last_give = remote(late.at[index], given_late, give_sems.at[5], take_sems.at[5], (s, partner))

        @pl.when(jnp.logical_not(edge))
        def _():
            pl.when(cross_halo)(lambda: wait_rim(far, index, recv_far.at[index, pieces + 1]))
            admit(pieces + 1)
            work(pieces)
            last_give.start()

        @pl.when(edge)
        def _():
            for i, at in enumerate((y * half_rim, yo * half_rim)):
                wait_rim(far, index, recv_far.at[index, pieces + 1 + i], half_rim)
                admit(pieces + 1, at, half_rim)
                work(pieces, at, half_rim)
            last_give.wait_recv()
            for t in range(n):
                column = jnp.where(z < n // 2, n - 1 - t, t)
                j = lax.rem(column, 2) + jnp.where(column // 2 == y, 0, 2)
                lanes_of = pl.ds(pl.multiple_of(j * width, width), width)
                value = (late[index, :, lanes_of] + given_late[:, lanes_of]).astype(BF16)
                tiles[2, t] = value.T.reshape(tiles.shape[2:])
                for half in range(2):
                    remote(tiles.at[2, t, half], recv.at[ns + s], tile_sems.at[0], tile_sems.at[1],
                           (2 * column + half, 2 * yo + 1)).start()

        finish()
        pack_far_band(1, known, known + 1)
        send_far_band(known, known + 1)
        project(pieces)
        forward.wait_send()
        pl.when(jnp.logical_not(edge))(last_give.wait_send)

    phase(0)
    phase(1)

    pl.when(c == 0)(lambda: sent(2 * pieces - 1, 0))
    pl.when(c == 1)(lambda: sent(2 * pieces + 1, 0))
    own.wait_send()
    pl.when(jnp.logical_not(edge))(plane_edge.wait_send)
    pl.when(plane_rim)(plane.wait_send)
    pl.when(cross_rim)(cross.wait_send)
    tile_bytes = remote(recv.at[pl.ds(0, ns)], recv.at[pl.ds(0, ns)], tile_sems.at[0], tile_sems.at[1],
                        (s, partner))
    own_tiles = recv.at[pl.ds(0, ns - 1)]
    remote(own_tiles, own_tiles, tile_sems.at[0], tile_sems.at[1], (s, partner)).wait_send()

    @pl.when(c == 0)
    def _():
        for order, first, last in ((0, 0, n - 1), (1, n - 1, n)):
            give(1, order, 2, first, last).wait_send()

    pl.when(c == 1)(tile_bytes.wait_send)
    pl.when(edge)(tile_bytes.wait_send)
    all_tiles = recv.at[pl.ds(0, 2 * ns - 1)]
    remote(all_tiles, all_tiles, tile_sems.at[0], tile_sems.at[1], (s, partner)).wait_recv()


def deliver(scale, weighted, modes, parts, weighted_out, modes_out, corr_out, corr, sems):
    pairs = ((weighted, weighted_out), (modes, modes_out), (corr, corr_out))
    copies = [pltpu.make_async_copy(held, target, sems.at[i]) for i, (held, target) in enumerate(pairs)]
    for copy in copies[:2]:
        copy.start()
    total = parts[0].astype(F32)
    for i in range(1, parts.shape[0]):
        total = total + parts[i].astype(F32)
    corr[...] = total * scale
    copies[2].start()
    for copy in copies:
        copy.wait()


def fast_shards(n, ns, snapshots, mass_blocks, neighbours, eigvecs):
    own_blocks, picks, size, _ = mass_blocks.shape
    total, width = snapshots.shape
    rows = total // n
    snaps = n * width
    pieces = own_blocks // HB
    sem = pltpu.SemaphoreType.DMA
    regular = pltpu.SemaphoreType.REGULAR
    vmem = pltpu.VMEM
    nz = ns // 2
    tile = snaps // ns
    held = own_blocks + 2 * HB
    modes_count = eigvecs.shape[1]
    hbm = pl.BlockSpec(memory_space=pltpu.HBM)
    inside = pl.BlockSpec(memory_space=pltpu.VMEM)
    block = (size, width)
    weighted, modes, parts = pl.pallas_call(
        functools.partial(fused, n, ns),
        out_shape=(jax.ShapeDtypeStruct((rows, snaps), BF16),
                   jax.ShapeDtypeStruct((rows, modes_count), BF16),
                   jax.ShapeDtypeStruct((2 * ns, tile, width), BF16)),
        in_specs=[hbm] * 4,
        out_specs=(inside, inside, inside),
        scratch_shapes=[
            vmem((2, held) + block, BF16), vmem((2, held) + block, BF16), vmem((held,) + block, BF16),
            vmem(mass_blocks.shape, BF16), vmem(eigvecs.shape, BF16),
            pltpu.SMEM((picks, own_blocks), jnp.int32), vmem((n, snaps, width), F32),
            vmem((2, width, snaps), F32), vmem((2, snaps, width), F32), vmem((width, snaps), F32),
            vmem((3, n, 2, tile, width), BF16),
            sem((5,)), sem, sem, sem((2,)), sem((2,)), sem((2, pieces + 3)), sem((3,)), sem((2,)),
            sem((6,)), sem((6,)), sem((2,)), regular, regular((nz,)),
        ],
        compiler_params=pltpu.CompilerParams(collective_id=0, has_side_effects=True,
                                             vmem_limit_bytes=40 * 2**20),
        name="fused",
    )(*(pltpu.with_memory_space_constraint(a, pltpu.HBM) for a in (
        neighbours.T, snapshots.reshape(total // size, size, width), mass_blocks, eigvecs)))
    weighted, modes, corr = pl.pallas_call(
        functools.partial(deliver, 1.0 / (total * ns)),
        out_shape=(pltpu.HBM(weighted.shape, BF16), pltpu.HBM(modes.shape, BF16), pltpu.HBM((tile, width), F32)),
        in_specs=[inside] * 3,
        out_specs=(hbm,) * 3,
        scratch_shapes=[vmem((tile, width), F32), sem((3,))],
        compiler_params=pltpu.CompilerParams(vmem_limit_bytes=2**20),
        name="deliver",
    )(*(pltpu.with_memory_space_constraint(a, pltpu.VMEM) for a in (weighted, modes, parts)))
    return weighted, corr.T, modes


def shifted(block, axis, distance):
    devices = range(lax.axis_size(axis))
    route = [(i - distance, i) for i in devices if i - distance in devices]
    return lax.ppermute(block, axis, route)


def plain_shards(snapshots, mass_blocks, neighbours, eigvecs):
    local_rows = lax.all_to_all(snapshots, "snap", split_axis=0, concat_axis=1, tiled=True)
    row_count, col_count = local_rows.shape
    block_size = mass_blocks.shape[2]
    rim_rows = HB * block_size
    below_rim = shifted(local_rows[row_count - rim_rows :], ("space", "snap"), 1)
    above_rim = shifted(local_rows[:rim_rows], ("space", "snap"), -1)
    extended = jnp.concatenate([below_rim, local_rows, above_rim], axis=0).reshape(
        -1, block_size, col_count
    )
    first_block = lax.axis_index(("space", "snap")) * (row_count // block_size)
    local_ids = neighbours - first_block + HB
    nearby = extended[local_ids]
    weighted = jnp.einsum("bjrc,bjcs->brs", mass_blocks, nearby, preferred_element_type=jnp.float32)
    weighted = weighted.reshape(row_count, col_count).astype(jnp.bfloat16)
    partial_corr = jnp.dot(weighted.T, local_rows, preferred_element_type=jnp.float32)
    band = lax.psum_scatter(partial_corr, "snap", scatter_dimension=0, tiled=True)
    correlation = lax.psum_scatter(band, "space", scatter_dimension=1, tiled=True)
    cell_total = row_count * lax.axis_size("space") * lax.axis_size("snap")
    correlation = correlation * (1.0 / cell_total)
    modes = jnp.dot(local_rows, eigvecs, preferred_element_type=jnp.float32).astype(jnp.bfloat16)
    return (weighted, correlation, modes)


def solution(mesh):
    n, ns = mesh.shape["snap"], mesh.shape["space"]

    def shards(snapshots, mass_blocks, neighbours, eigvecs):
        width = snapshots.shape[1]
        own_blocks, _, size, _ = mass_blocks.shape
        rows = own_blocks * size
        whole = n == 4 and ns == 2 * n and width % 128 == 0 and width == size
        if whole and snapshots.shape[0] == n * rows and own_blocks % HB == 0 and own_blocks >= 4 * HB:
            return fast_shards(n, ns, snapshots, mass_blocks, neighbours, eigvecs)
        return plain_shards(snapshots, mass_blocks, neighbours, eigvecs)

    in_specs = (
        P("space", "snap"),
        P(("space", "snap"), None, None, None),
        P(("space", "snap"), None),
        P(),
    )
    out_specs = (P(("space", "snap"), None), P("snap", "space"), P(("space", "snap"), None))
    return jax.shard_map(shards, mesh=mesh, in_specs=in_specs, out_specs=out_specs, check_vma=False)
```
